32 devices in a mesh: tm: 4 (over z), height: 4 (over y, x), width: 2 (over core).
Axes of the slice: x: 2, y: 2, z: 4, core: 2. Of those that a mesh axis runs over, the one named last changes fastest.
Arguments:
- frames: bfloat16 [8, 64, 32, 384], P('tm', 'height', 'width'), may hold values from -20 to 20
- attn_gain: float32 [384], replicated, may hold values from 0.25 to 1.75
- qkv_weight: bfloat16 [384, 1152], replicated, may hold values from -2 to 2
- proj_weight: bfloat16 [384, 384], replicated, may hold values from -0.3125 to 0.3125
- proj_bias: float32 [384], replicated, may hold values from -1.5 to 1.5
- conv_gain: float32 [384], replicated, may hold values from 0.25 to 1.75
- conv_weight: bfloat16 [3, 3, 3, 384, 384], replicated, may hold values from -0.0625 to 0.0625
- conv_bias: float32 [384], replicated, may hold values from -1.5 to 1.5
Outputs:
- decoded: bfloat16 [8, 64, 32, 384], P('tm', 'height', 'width')
The draws below stay inside these ranges and needn't reach their ends.
All inputs are finite; a program needn't handle non-finite values.
Results may differ from the reference program's by a relative error of at most 0.011.
Values may be sent and summed in bfloat16 or wider, within the bound.
A program may use at most 128 MiB of HBM per device.

```python
import math
import jax
import jax.numpy as jnp
from jax import lax

C = 384
FRAMES = 8
HEIGHT_CELLS = 64
WIDTH_CELLS = 32


def draw_frames(key, part):
    first = jax.random.fold_in(jax.random.fold_in(key, 11), 0)
    shape_all = (FRAMES, HEIGHT_CELLS, WIDTH_CELLS, C)
    base = jax.random.normal(first, shape_all, jnp.float32)
    return jnp.clip(base, -20.0, 20.0).astype(jnp.bfloat16)


def draw_qkv_weight(key, part):
    first = jax.random.fold_in(jax.random.fold_in(key, 23), 0)
    third = jax.random.fold_in(jax.random.fold_in(key, 23), 2)
    fourth = jax.random.fold_in(jax.random.fold_in(key, 23), 3)
    root_scale = C ** (-0.5)
    query_part = 1.6 * root_scale * jax.random.normal(first, (C, C), jnp.float32)
    key_part = 1.6 * root_scale * jax.random.normal(third, (C, C), jnp.float32)
    value_part = root_scale * jax.random.normal(fourth, (C, C), jnp.float32)
    return jnp.clip(jnp.concatenate([query_part, key_part, value_part], axis=1), -2.0, 2.0).astype(jnp.bfloat16)


def normal_values(key, extent, width, bound, held_as=jnp.bfloat16):
    values = width * jax.random.normal(key, extent, jnp.float32)
    return jnp.clip(values, min=-bound, max=bound).astype(held_as)


def setup_inputs(seed: int = 0) -> dict:
    arg_keys = jax.random.split(jax.random.key(seed), 9)
    return {
        "frames": draw_frames(jax.random.fold_in(arg_keys[8], 71), 0),
        "attn_gain": jnp.clip(1.0 + 0.15 * jax.random.normal(arg_keys[1], (C,), jnp.float32), 0.25, 1.75),
        "qkv_weight": draw_qkv_weight(jax.random.fold_in(arg_keys[8], 71), 0),
        "proj_weight": normal_values(arg_keys[3], (C, C), C ** -0.5, 0.3125),
        "proj_bias": normal_values(arg_keys[4], (C,), 0.3, 1.5, jnp.float32),
        "conv_gain": jnp.clip(1.0 + 0.15 * jax.random.normal(arg_keys[5], (C,), jnp.float32), 0.25, 1.75),
        "conv_weight": normal_values(arg_keys[6], (3, 3, 3, C, C), (27 * C) ** -0.5, 0.0625),
        "conv_bias": normal_values(arg_keys[7], (C,), 0.3, 1.5, jnp.float32),
    }


epsilon = 1e-06

def rms_scale(values, gain_row):
    widened = values.astype(jnp.float32)
    mean_square = lax.optimization_barrier(jnp.mean(widened * widened, axis=-1, keepdims=True))
    return widened * lax.rsqrt(mean_square + epsilon) * gain_row

def reference(frames, attn_gain, qkv_weight, proj_weight, proj_bias, conv_gain, conv_weight, conv_bias):
    frame_count, height_rows, width_cols, channels = frames.shape
    flattened = frames.reshape(frame_count, height_rows * width_cols, channels)
    attn_in = rms_scale(flattened, attn_gain).astype(jnp.bfloat16)
    score_scale = 1.0 / math.sqrt(channels)

    def one_frame(frame_in):
        projected = jnp.dot(frame_in, qkv_weight, preferred_element_type=jnp.float32).astype(jnp.bfloat16)
        queries = projected[:, :channels]
        key_block = projected[:, channels:2 * channels]
        value_block = projected[:, 2 * channels:]
        scores = jnp.dot(queries, key_block.T, preferred_element_type=jnp.float32) * score_scale
        row_max = lax.optimization_barrier(jnp.max(scores, axis=-1, keepdims=True))
        weights = jnp.exp(scores - row_max)
        row_sum = lax.optimization_barrier(jnp.sum(weights, axis=-1, keepdims=True))
        summed = jnp.dot(weights.astype(jnp.bfloat16), value_block, preferred_element_type=jnp.float32)
        return (summed / row_sum).astype(jnp.bfloat16)
    attended = lax.map(one_frame, attn_in)
    projected_out = jnp.dot(attended.reshape(-1, channels), proj_weight, preferred_element_type=jnp.float32)
    mixed = (flattened.reshape(-1, channels).astype(jnp.float32) + projected_out + proj_bias).astype(jnp.bfloat16)
    conv_in = jax.nn.silu(rms_scale(mixed, conv_gain)).astype(jnp.bfloat16)
    conv_in = conv_in.reshape(frame_count, height_rows, width_cols, channels)
    padded = jnp.pad(conv_in, ((2, 0), (1, 1), (1, 1), (0, 0)))
    conv_out = jnp.zeros((frame_count * height_rows * width_cols, channels), jnp.float32)
    for step_t in range(3):
        for step_h in range(3):
            for step_w in range(3):
                window = padded[step_t:step_t + frame_count, step_h:step_h + height_rows, step_w:step_w + width_cols]
                conv_out = conv_out + jnp.dot(window.reshape(-1, channels), conv_weight[step_t, step_h, step_w], preferred_element_type=jnp.float32)
    decoded = mixed.astype(jnp.float32) + conv_out + conv_bias
    return decoded.astype(jnp.bfloat16).reshape(frame_count, height_rows, width_cols, channels)
```

```python
import functools
import math

import jax
import jax.numpy as jnp
from jax import lax
from jax.experimental import pallas as pl
from jax.experimental.pallas import tpu as pltpu
from jax.sharding import PartitionSpec as P

epsilon = 1e-06
MESH = pl.DeviceIdType.MESH
f32 = jnp.float32
bf16 = jnp.bfloat16
lanes = 128

MOVES = [
    (dt, dh, dw)
    for dt in (1, 0)
    for dh in (0, -1, 1)
    for dw in (0, -1, 1)
    if (dt, dh, dw) != (0, 0, 0)
]
CORNERS = {(-1, -1): 0, (-1, 1): 1, (1, -1): 2, (1, 1): 3}


def dot(a, b):
    return jnp.dot(a, b, preferred_element_type=f32)


def dot_t(a, b):
    return lax.dot_general(a, b, (((1,), (1,)), ((), ())), preferred_element_type=f32)


def rms(values, gain_row):
    mean_square = jnp.mean(values * values, axis=-1, keepdims=True)
    return values * lax.rsqrt(mean_square + epsilon) * gain_row


def kernel(
    sizes,
    frames_hbm,
    qkv_hbm,
    proj_hbm,
    convw_hbm,
    attn_gain,
    proj_bias,
    conv_gain,
    conv_bias,
    out_ref,
    frames_v,
    qkv_v,
    proj_v,
    convw_v,
    gathered,
    query,
    value_proj,
    scores,
    weights,
    conv_f32,
    mixed,
    centre,
    columns,
    corners,
    edge,
    shifted,
    total,
    load_sem,
    convw_sem,
    ring_send,
    ring_recv,
    side_send,
    side_recv,
    halo_send,
    halo_recv,
):
    T, H, W, rows, cols, channels = sizes
    cells = rows * cols
    half = cells // 2
    blocks = H * W
    t, h, w = lax.axis_index("tm"), lax.axis_index("height"), lax.axis_index("width")

    loads = [
        pltpu.make_async_copy(frames_hbm, frames_v, load_sem.at[0]),
        pltpu.make_async_copy(qkv_hbm, qkv_v, load_sem.at[1]),
        pltpu.make_async_copy(proj_hbm, proj_v, load_sem.at[2]),
    ]
    for copy in loads:
        copy.start()
    convw_loads = [
        pltpu.make_async_copy(convw_hbm.at[pl.ds(3 * a, 3)], convw_v.at[pl.ds(3 * a, 3)], convw_sem.at[a])
        for a in range(3)
    ]
    for copy in convw_loads:
        copy.start()

    square = H == 4 and W == 2

    def turn(p):
        return p + (p // 2) * (1 - 2 * (p % 2)) if square else p

    pos = turn(h)

    def at_pos(offset):
        return turn((pos + offset + H) % H)

    def device(dt, hh, ww):
        return {"tm": t + dt, "height": hh, "width": ww}

    def inside(dt, dh, dw):
        ok = None
        for value, delta, count in ((t, dt, T), (h, dh, H), (w, dw, W)):
            if delta:
                one = value + delta < count if delta > 0 else value + delta >= 0
                ok = one if ok is None else jnp.logical_and(ok, one)
        return ok

    centre[...] = jnp.zeros_like(centre)
    columns[...] = jnp.zeros_like(columns)
    corners[...] = jnp.zeros_like(corners)

    barrier = pltpu.get_barrier_semaphore()

    def greet(target):
        pl.semaphore_signal(barrier, inc=1, device_id=target, device_id_type=MESH)

    close = 0
    if H > 1:
        greet(device(0, at_pos(1), w))
        greet(device(0, at_pos(-1), w))
        close += 2
    for j in range(1, W):
        greet(device(0, h, (w + j) % W))
        close += 1
    for dt, dh, dw in MOVES:
        @pl.when(inside(-dt, -dh, -dw))
        def _():
            greet(device(-dt, h - dh, w - dw))

    own = h * W + w
    loads[0].wait()
    for f in (1, 0):
        gathered[f, own] = rms(frames_v[f].astype(f32), attn_gain[...]).astype(bf16)

    def count(delta, value, limit):
        one = value + delta < limit if delta > 0 else value + delta >= 0
        return jnp.where(one, 1, 0)

    around = (1 + count(1, h, H) + count(-1, h, H)) * (1 + count(1, w, W) + count(-1, w, W))
    pl.semaphore_wait(barrier, close + around - 1 + count(1, t, T) * around)

    def ring_copy(f, way, step, part):
        sign = 1 if way == 0 else -1
        origin = at_pos(-sign * (step - 1))
        piece = gathered.at[f, origin * W + w, pl.ds(part * half, half)]
        return pltpu.make_async_remote_copy(
            piece,
            piece,
            ring_send.at[f, way, step - 1, part],
            ring_recv.at[f, way, step - 1, part],
            device_id=device(0, at_pos(sign), w),
            device_id_type=MESH,
        )

    def ring_arrival(f, way, step, part):
        sign = 1 if way == 0 else -1
        origin = at_pos(-sign * step)
        piece = gathered.at[f, origin * W + w, pl.ds(part * half, half)]
        return pltpu.make_async_remote_copy(
            piece,
            piece,
            ring_send.at[f, way, step - 1, part],
            ring_recv.at[f, way, step - 1, part],
            device_id=device(0, at_pos(sign), w),
            device_id_type=MESH,
        )

    def parts_of(way, step):
        if 2 * step < H:
            return (0, 1) if way == 0 else (1, 0)
        return (way,)

    def side_copy(f, offset, part, j, incoming=False):
        column = (w - j + W) % W if incoming else w
        piece = gathered.at[f, at_pos(-offset) * W + column, pl.ds(part * half, half)]
        return pltpu.make_async_remote_copy(
            piece,
            piece,
            side_send.at[f, offset, part, j],
            side_recv.at[f, offset, part, j],
            device_id=device(0, h, (w + j) % W),
            device_id_type=MESH,
        )

    def pass_aside(f, offset, part):
        for j in range(1, W):
            side_copy(f, offset, part, j).start()

    steps = H // 2

    def start_own(f):
        if H > 1:
            for k in range(len(parts_of(0, 1))):
                for way in (0, 1):
                    ring_copy(f, way, 1, parts_of(way, 1)[k]).start()
        for part in (0, 1):
            pass_aside(f, 0, part)

    def arrive(f, way, step, k):
        part = parts_of(way, step)[k]
        ring_arrival(f, way, step, part).wait_recv()
        if step < steps and part in parts_of(way, step + 1):
            ring_copy(f, way, step + 1, part).start()
        pass_aside(f, step if way == 0 else H - step, part)

    arrivals = [
        (step, k, way)
        for step in range(1, steps + 1)
        for k in range(len(parts_of(0, step)))
        for way in (0, 1)
    ]

    def finish_gather(f):
        for offset in range(H):
            for part in (0, 1):
                for j in range(1, W):
                    side_copy(f, offset, part, j, incoming=True).wait_recv()

    start_own(1)

    loads[1].wait()
    loads[2].wait()
    value_proj[...] = dot(qkv_v[:, 2 * channels :], proj_v[...]).astype(bf16)
    score_scale = 1.0 / math.sqrt(channels)
    for f in (1, 0):
        q = dot(gathered[f, own], qkv_v[:, :channels]).astype(bf16)
        query[f] = (dot_t(q, qkv_v[:, channels : 2 * channels]) * score_scale).astype(bf16)

    group = math.gcd(blocks, 8)

    def attend(f):
        q = query[f]
        lane_max = None
        for j in range(blocks):
            s = dot_t(q, gathered[f, j])
            scores[:, j * cells : (j + 1) * cells] = s
            for c in range(0, cells, lanes):
                part = s[:, c : c + lanes]
                lane_max = part if lane_max is None else jnp.maximum(lane_max, part)
        row_max = jnp.max(lane_max, axis=-1, keepdims=True)
        lane_sum = None
        summed = None
        for g in range(0, blocks, group):
            for j in range(g, g + group):
                p = jnp.exp(scores[:, j * cells : (j + 1) * cells] - row_max)
                for c in range(0, cells, lanes):
                    part = p[:, c : c + lanes]
                    lane_sum = part if lane_sum is None else lane_sum + part
                weights[:, (j - g) * cells : (j - g + 1) * cells] = p.astype(bf16)
            keys = gathered[f, pl.ds(g, group)].reshape(group * cells, channels)
            one = dot(weights[...], keys)
            summed = one if summed is None else summed + one
        row_sum = jnp.sum(lane_sum, axis=-1, keepdims=True)
        context = (summed / row_sum).astype(bf16)
        projected = dot(context, value_proj[...])
        now = (frames_v[f].astype(f32) + projected + proj_bias[...]).astype(bf16)
        mixed[f] = now
        v = rms(now.astype(f32), conv_gain[...])
        c_in = v / (1.0 + jnp.exp(-v))
        centre[2 + f, pl.ds(cols, cells)] = c_in.astype(bf16)
        for c in range(channels // lanes):
            span = slice(c * lanes, (c + 1) * lanes)
            conv_f32[c] = c_in[:, span]
            edge[f, 0, :, span] = conv_f32[c, pl.ds(0, rows, cols), :].astype(bf16)
            edge[f, 1, :, span] = conv_f32[c, pl.ds(cols - 1, rows, cols), :].astype(bf16)

    def halo_copy(f, index):
        dt, dh, dw = MOVES[index]
        slot = f if dt else 2 + f
        row = {0: cols, -1: cols, 1: rows * cols}[dh]
        if dh == 0 and dw == 0:
            src = centre.at[2 + f, pl.ds(cols, cells)]
            dst = centre.at[slot, pl.ds(cols, cells)]
        elif dw == 0:
            src = centre.at[2 + f, pl.ds(row, cols)]
            dst = centre.at[slot, pl.ds((rows + 1) * cols if dh < 0 else 0, cols)]
        elif dh == 0:
            src = edge.at[f, 0 if dw < 0 else 1]
            dst = columns.at[slot, 1 if dw < 0 else 0]
        else:
            src = centre.at[2 + f, pl.ds(row, cols)]
            dst = corners.at[slot, CORNERS[(-dh, -dw)]]
        return pltpu.make_async_remote_copy(
            src,
            dst,
            halo_send.at[f, index],
            halo_recv.at[f, index],
            device_id=device(dt, h + dh, w + dw),
            device_id_type=MESH,
        )

    def send_halos(f):
        for index, move in enumerate(MOVES):
            @pl.when(inside(*move))
            def _():
                halo_copy(f, index).start()

    def wait_halos(f, ahead):
        for index, (dt, dh, dw) in enumerate(MOVES):
            if dt == ahead:
                @pl.when(inside(-dt, -dh, -dw))
                def _():
                    halo_copy(f, index).wait_recv()

    def shift(s):
        place = lax.broadcasted_iota(jnp.int32, (cols, channels), 0)
        first, last = place == 0, place == cols - 1
        low, high = columns[s, 0].astype(f32), columns[s, 1].astype(f32)
        for r in range(rows + 2):
            here = centre[s, r * cols : (r + 1) * cols]
            x = here.astype(f32)
            if 0 < r <= rows:
                before, after = low[r - 1 : r], high[r - 1 : r]
            else:
                c = 0 if r == 0 else 2
                before = corners[s, c].astype(f32)[cols - 1 : cols]
                after = corners[s, c + 1].astype(f32)[0:1]
            there = pl.ds(r * cols, cols)
            shifted[s, there, 0:channels] = jnp.where(
                first, before, pltpu.roll(x, 1, axis=0)
            ).astype(bf16)
            shifted[s, there, channels : 2 * channels] = here
            shifted[s, there, 2 * channels : 3 * channels] = jnp.where(
                last, after, pltpu.roll(x, cols - 1, axis=0)
            ).astype(bf16)

    def conv(o, a):
        s = o + a
        value = None
        for b in range(3):
            one = dot(shifted[s, b * cols : b * cols + cells], convw_v[3 * a + b])
            value = one if value is None else value + one
        return value

    early = 2 if steps > 1 else 0
    for step, k, way in arrivals[:early]:
        arrive(1, way, step, k)
    start_own(0)
    for step, k, way in arrivals[early:]:
        arrive(1, way, step, k)
    finish_gather(1)
    for step, k, way in arrivals[:early]:
        arrive(0, way, step, k)
    attend(1)
    send_halos(1)
    for copy in convw_loads:
        copy.wait()
    for step, k, way in arrivals[early : 2 * early]:
        arrive(0, way, step, k)
    wait_halos(1, 0)
    shift(3)
    total[1] = conv(1, 2)
    for step, k, way in arrivals[2 * early :]:
        arrive(0, way, step, k)
    finish_gather(0)
    attend(0)
    send_halos(0)
    wait_halos(0, 0)
    shift(2)
    total[0] = conv(0, 2)
    total[1] += conv(1, 1)
    wait_halos(1, 1)
    shift(1)
    total[0] += conv(0, 1)
    total[1] += conv(1, 0)
    out_ref[1] = (mixed[1].astype(f32) + total[1] + conv_bias[...]).astype(bf16)
    wait_halos(0, 1)
    shift(0)
    out_ref[0] = (
        mixed[0].astype(f32) + (total[0] + conv(0, 0)) + conv_bias[...]
    ).astype(bf16)

    for f in (1, 0):
        for step in range(1, steps + 1):
            for way in (0, 1):
                for part in parts_of(way, step):
                    ring_copy(f, way, step, part).wait_send()
        for offset in range(H):
            for part in (0, 1):
                for j in range(1, W):
                    side_copy(f, offset, part, j).wait_send()
        for index, move in enumerate(MOVES):
            @pl.when(inside(*move))
            def _():
                halo_copy(f, index).wait_send()


def shards(
    mesh_sizes,
    frames,
    attn_gain,
    qkv_weight,
    proj_weight,
    proj_bias,
    conv_gain,
    conv_weight,
    conv_bias,
):
    T, H, W = mesh_sizes
    frame_count, rows, cols, channels = frames.shape
    cells = rows * cols
    blocks = H * W
    group = math.gcd(blocks, 8)
    anywhere = pl.BlockSpec(memory_space=pl.ANY)
    vmem = pl.BlockSpec(memory_space=pltpu.VMEM)
    dma = pltpu.SemaphoreType.DMA
    steps = max(H // 2, 1)
    decoded = pl.pallas_call(
        functools.partial(kernel, (T, H, W, rows, cols, channels)),
        out_shape=jax.ShapeDtypeStruct((frame_count, cells, channels), bf16),
        in_specs=[anywhere] * 4 + [vmem] * 4,
        out_specs=vmem,
        scratch_shapes=[
            pltpu.VMEM((2, cells, channels), bf16),
            pltpu.VMEM((channels, 3 * channels), bf16),
            pltpu.VMEM((channels, channels), bf16),
            pltpu.VMEM((9, 3 * channels, channels), bf16),
            pltpu.VMEM((2, blocks, cells, channels), bf16),
            pltpu.VMEM((2, cells, channels), bf16),
            pltpu.VMEM((channels, channels), bf16),
            pltpu.VMEM((cells, blocks * cells), f32),
            pltpu.VMEM((cells, group * cells), bf16),
            pltpu.VMEM((channels // lanes, cells, lanes), f32),
            pltpu.VMEM((2, cells, channels), bf16),
            pltpu.VMEM((4, (rows + 2) * cols, channels), bf16),
            pltpu.VMEM((4, 2, rows, channels), bf16),
            pltpu.VMEM((4, 4, cols, channels), bf16),
            pltpu.VMEM((2, 2, rows, channels), bf16),
            pltpu.VMEM((4, (rows + 2) * cols, 3 * channels), bf16),
            pltpu.VMEM((2, cells, channels), f32),
            dma((3,)),
            dma((3,)),
            dma((2, 2, steps, 2)),
            dma((2, 2, steps, 2)),
            dma((2, H, 2, W)),
            dma((2, H, 2, W)),
            dma((2, len(MOVES))),
            dma((2, len(MOVES))),
        ],
        compiler_params=pltpu.CompilerParams(
            collective_id=0, has_side_effects=True, vmem_limit_bytes=60 * 2**20
        ),
    )(
        frames.reshape(frame_count, cells, channels),
        qkv_weight,
        proj_weight,
        conv_weight.reshape(9, 3 * channels, channels),
        attn_gain.reshape(1, channels),
        proj_bias.reshape(1, channels),
        conv_gain.reshape(1, channels),
        conv_bias.reshape(1, channels),
    )
    return decoded.reshape(frame_count, rows, cols, channels)


def solution(mesh):
    sizes = tuple(mesh.shape[axis] for axis in ("tm", "height", "width"))
    in_specs = (P("tm", "height", "width", None), P(), P(), P(), P(), P(), P(), P())
    out_specs = P("tm", "height", "width", None)
    return jax.shard_map(
        functools.partial(shards, sizes),
        mesh=mesh,
        in_specs=in_specs,
        out_specs=out_specs,
        check_vma=False,
    )
```

```python
import functools
import math

import jax
import jax.numpy as jnp
from jax import lax
from jax.experimental import pallas as pl
from jax.experimental.pallas import tpu as pltpu
from jax.sharding import PartitionSpec as P

epsilon = 1e-06
MESH = pl.DeviceIdType.MESH
f32 = jnp.float32
bf16 = jnp.bfloat16
lanes = 128

MOVES = [
    (dt, dh, dw)
    for dt in (1, 0)
    for dh in (0, -1, 1)
    for dw in (0, -1, 1)
    if (dt, dh, dw) != (0, 0, 0)
]
CORNERS = {(-1, -1): 0, (-1, 1): 1, (1, -1): 2, (1, 1): 3}


def dot(a, b):
    return jnp.dot(a, b, preferred_element_type=f32)


def dot_t(a, b):
    return lax.dot_general(a, b, (((1,), (1,)), ((), ())), preferred_element_type=f32)


def row(vector):
    return vector[...].reshape(1, vector.shape[0])


def rms(values, gain_row):
    mean_square = jnp.mean(values * values, axis=-1, keepdims=True)
    return values * lax.rsqrt(mean_square + epsilon) * gain_row


def kernel(
    sizes,
    frames_hbm,
    qkv_hbm,
    proj_hbm,
    convw_hbm,
    attn_gain_hbm,
    proj_bias_hbm,
    conv_gain_hbm,
    conv_bias_hbm,
    out_hbm,
    attn_gain,
    proj_bias,
    conv_gain,
    conv_bias,
    out_v,
    frames_v,
    qkv_v,
    proj_v,
    convw_v,
    gathered,
    query,
    value_proj,
    scores,
    weights,
    conv_f32,
    mixed,
    centre,
    columns,
    corners,
    edge,
    shifted,
    total,
    load_sem,
    out_sem,
    convw_sem,
    ring_send,
    ring_recv,
    side_send,
    side_recv,
    halo_send,
    halo_recv,
):
    T, H, W, rows, cols, channels = sizes
    cells = rows * cols
    half = cells // 2
    blocks = H * W
    t, h, w = lax.axis_index("tm"), lax.axis_index("height"), lax.axis_index("width")

    loads = [
        pltpu.make_async_copy(frames_hbm, frames_v, load_sem.at[0]),
        pltpu.make_async_copy(attn_gain_hbm, attn_gain, load_sem.at[1]),
        pltpu.make_async_copy(qkv_hbm, qkv_v, load_sem.at[2]),
        pltpu.make_async_copy(proj_hbm, proj_v, load_sem.at[3]),
        pltpu.make_async_copy(proj_bias_hbm, proj_bias, load_sem.at[4]),
        pltpu.make_async_copy(conv_gain_hbm, conv_gain, load_sem.at[5]),
        pltpu.make_async_copy(conv_bias_hbm, conv_bias, load_sem.at[6]),
    ]
    for copy in loads:
        copy.start()
    convw_loads = [
        pltpu.make_async_copy(convw_hbm.at[pl.ds(3 * a, 3)], convw_v.at[pl.ds(3 * a, 3)], convw_sem.at[a])
        for a in range(3)
    ]

    square = H == 4 and W == 2

    def turn(p):
        return p + (p // 2) * (1 - 2 * (p % 2)) if square else p

    pos = turn(h)

    def at_pos(offset):
        return turn((pos + offset + H) % H)

    def device(dt, hh, ww):
        return {"tm": t + dt, "height": hh, "width": ww}

    def inside(dt, dh, dw):
        ok = None
        for value, delta, count in ((t, dt, T), (h, dh, H), (w, dw, W)):
            if delta:
                one = value + delta < count if delta > 0 else value + delta >= 0
                ok = one if ok is None else jnp.logical_and(ok, one)
        return ok

    centre[...] = jnp.zeros_like(centre)
    columns[...] = jnp.zeros_like(columns)
    corners[...] = jnp.zeros_like(corners)

    barrier = pltpu.get_barrier_semaphore()

    def greet(target):
        pl.semaphore_signal(barrier, inc=1, device_id=target, device_id_type=MESH)

    close = 0
    if H > 1:
        greet(device(0, at_pos(1), w))
        greet(device(0, at_pos(-1), w))
        close += 2
    for j in range(1, W):
        greet(device(0, h, (w + j) % W))
        close += 1
    for dt, dh, dw in MOVES:
        @pl.when(inside(-dt, -dh, -dw))
        def _():
            greet(device(-dt, h - dh, w - dw))

    own = h * W + w
    loads[0].wait()
    loads[1].wait()
    for f in (1, 0):
        gathered[f, own] = rms(frames_v[f].astype(f32), row(attn_gain)).astype(bf16)

    def count(delta, value, limit):
        one = value + delta < limit if delta > 0 else value + delta >= 0
        return jnp.where(one, 1, 0)

    around = (1 + count(1, h, H) + count(-1, h, H)) * (1 + count(1, w, W) + count(-1, w, W))
    pl.semaphore_wait(barrier, close + around - 1 + count(1, t, T) * around)

    def ring_copy(f, way, step, part):
        sign = 1 if way == 0 else -1
        origin = at_pos(-sign * (step - 1))
        piece = gathered.at[f, origin * W + w, pl.ds(part * half, half)]
        return pltpu.make_async_remote_copy(
            piece,
            piece,
            ring_send.at[f, way, step - 1, part],
            ring_recv.at[f, way, step - 1, part],
            device_id=device(0, at_pos(sign), w),
            device_id_type=MESH,
        )

    def ring_arrival(f, way, step, part):
        sign = 1 if way == 0 else -1
        origin = at_pos(-sign * step)
        piece = gathered.at[f, origin * W + w, pl.ds(part * half, half)]
        return pltpu.make_async_remote_copy(
            piece,
            piece,
            ring_send.at[f, way, step - 1, part],
            ring_recv.at[f, way, step - 1, part],
            device_id=device(0, at_pos(sign), w),
            device_id_type=MESH,
        )

    def parts_of(way, step):
        if 2 * step < H:
            return (0, 1) if way == 0 else (1, 0)
        return (way,)

    def side_copy(f, offset, part, j, incoming=False):
        column = (w - j + W) % W if incoming else w
        piece = gathered.at[f, at_pos(-offset) * W + column, pl.ds(part * half, half)]
        return pltpu.make_async_remote_copy(
            piece,
            piece,
            side_send.at[f, offset, part, j],
            side_recv.at[f, offset, part, j],
            device_id=device(0, h, (w + j) % W),
            device_id_type=MESH,
        )

    def pass_aside(f, offset, part):
        for j in range(1, W):
            side_copy(f, offset, part, j).start()

    steps = H // 2

    def start_own(f):
        if H > 1:
            for k in range(len(parts_of(0, 1))):
                for way in (0, 1):
                    ring_copy(f, way, 1, parts_of(way, 1)[k]).start()
        for part in (0, 1):
            pass_aside(f, 0, part)

    def arrive(f, way, step, k):
        part = parts_of(way, step)[k]
        ring_arrival(f, way, step, part).wait_recv()
        if step < steps and part in parts_of(way, step + 1):
            ring_copy(f, way, step + 1, part).start()
        pass_aside(f, step if way == 0 else H - step, part)

    arrivals = [
        (step, k, way)
        for step in range(1, steps + 1)
        for k in range(len(parts_of(0, step)))
        for way in (0, 1)
    ]

    def finish_gather(f):
        for offset in range(H):
            for part in (0, 1):
                for j in range(1, W):
                    side_copy(f, offset, part, j, incoming=True).wait_recv()

    start_own(1)
    for copy in convw_loads:
        copy.start()

    for copy in loads[2:]:
        copy.wait()
    value_proj[...] = dot(qkv_v[:, 2 * channels :], proj_v[...]).astype(bf16)
    score_scale = 1.0 / math.sqrt(channels)
    for f in (1, 0):
        q = dot(gathered[f, own], qkv_v[:, :channels]).astype(bf16)
        query[f] = (dot_t(q, qkv_v[:, channels : 2 * channels]) * score_scale).astype(bf16)

    group = math.gcd(blocks, 8)

    def attend(f):
        q = query[f]
        lane_max = None
        for j in range(blocks):
            s = dot_t(q, gathered[f, j])
            scores[:, j * cells : (j + 1) * cells] = s
            for c in range(0, cells, lanes):
                part = s[:, c : c + lanes]
                lane_max = part if lane_max is None else jnp.maximum(lane_max, part)
        row_max = jnp.max(lane_max, axis=-1, keepdims=True)
        lane_sum = None
        summed = None
        for g in range(0, blocks, group):
            for j in range(g, g + group):
                p = jnp.exp(scores[:, j * cells : (j + 1) * cells] - row_max)
                for c in range(0, cells, lanes):
                    part = p[:, c : c + lanes]
                    lane_sum = part if lane_sum is None else lane_sum + part
                weights[:, (j - g) * cells : (j - g + 1) * cells] = p.astype(bf16)
            keys = gathered[f, pl.ds(g, group)].reshape(group * cells, channels)
            one = dot(weights[...], keys)
            summed = one if summed is None else summed + one
        row_sum = jnp.sum(lane_sum, axis=-1, keepdims=True)
        context = (summed / row_sum).astype(bf16)
        projected = dot(context, value_proj[...])
        now = (frames_v[f].astype(f32) + projected + row(proj_bias)).astype(bf16)
        mixed[f] = now
        v = rms(now.astype(f32), row(conv_gain))
        c_in = v / (1.0 + jnp.exp(-v))
        centre[2 + f, pl.ds(cols, cells)] = c_in.astype(bf16)
        for c in range(channels // lanes):
            span = slice(c * lanes, (c + 1) * lanes)
            conv_f32[c] = c_in[:, span]
            edge[f, 0, :, span] = conv_f32[c, pl.ds(0, rows, cols), :].astype(bf16)
            edge[f, 1, :, span] = conv_f32[c, pl.ds(cols - 1, rows, cols), :].astype(bf16)

    def halo_copy(f, index):
        dt, dh, dw = MOVES[index]
        slot = f if dt else 2 + f
        row = {0: cols, -1: cols, 1: rows * cols}[dh]
        if dh == 0 and dw == 0:
            src = centre.at[2 + f, pl.ds(cols, cells)]
            dst = centre.at[slot, pl.ds(cols, cells)]
        elif dw == 0:
            src = centre.at[2 + f, pl.ds(row, cols)]
            dst = centre.at[slot, pl.ds((rows + 1) * cols if dh < 0 else 0, cols)]
        elif dh == 0:
            src = edge.at[f, 0 if dw < 0 else 1]
            dst = columns.at[slot, 1 if dw < 0 else 0]
        else:
            src = centre.at[2 + f, pl.ds(row, cols)]
            dst = corners.at[slot, CORNERS[(-dh, -dw)]]
        return pltpu.make_async_remote_copy(
            src,
            dst,
            halo_send.at[f, index],
            halo_recv.at[f, index],
            device_id=device(dt, h + dh, w + dw),
            device_id_type=MESH,
        )

    def send_halos(f):
        for index, move in enumerate(MOVES):
            @pl.when(inside(*move))
            def _():
                halo_copy(f, index).start()

    def wait_halos(f, ahead):
        for index, (dt, dh, dw) in enumerate(MOVES):
            if dt == ahead:
                @pl.when(inside(-dt, -dh, -dw))
                def _():
                    halo_copy(f, index).wait_recv()

    def shift(s):
        place = lax.broadcasted_iota(jnp.int32, (cols, channels), 0)
        first, last = place == 0, place == cols - 1
        low, high = columns[s, 0].astype(f32), columns[s, 1].astype(f32)
        for r in range(rows + 2):
            here = centre[s, r * cols : (r + 1) * cols]
            x = here.astype(f32)
            if 0 < r <= rows:
                before, after = low[r - 1 : r], high[r - 1 : r]
            else:
                c = 0 if r == 0 else 2
                before = corners[s, c].astype(f32)[cols - 1 : cols]
                after = corners[s, c + 1].astype(f32)[0:1]
            there = pl.ds(r * cols, cols)
            shifted[s, there, 0:channels] = jnp.where(
                first, before, pltpu.roll(x, 1, axis=0)
            ).astype(bf16)
            shifted[s, there, channels : 2 * channels] = here
            shifted[s, there, 2 * channels : 3 * channels] = jnp.where(
                last, after, pltpu.roll(x, cols - 1, axis=0)
            ).astype(bf16)

    def conv(o, a):
        s = o + a
        value = None
        for b in range(3):
            one = dot(shifted[s, b * cols : b * cols + cells], convw_v[3 * a + b])
            value = one if value is None else value + one
        return value

    def out_copy(f):
        return pltpu.make_async_copy(out_v.at[f], out_hbm.at[f], out_sem.at[f])

    early = 2 if steps > 1 else 0
    for step, k, way in arrivals[:early]:
        arrive(1, way, step, k)
    start_own(0)
    for step, k, way in arrivals[early:]:
        arrive(1, way, step, k)
    finish_gather(1)
    for step, k, way in arrivals[:early]:
        arrive(0, way, step, k)
    attend(1)
    send_halos(1)
    for copy in convw_loads:
        copy.wait()
    for step, k, way in arrivals[early : 2 * early]:
        arrive(0, way, step, k)
    wait_halos(1, 0)
    shift(3)
    total[1] = conv(1, 2)
    for step, k, way in arrivals[2 * early :]:
        arrive(0, way, step, k)
    finish_gather(0)
    attend(0)
    send_halos(0)
    wait_halos(0, 0)
    shift(2)
    total[0] = conv(0, 2)
    total[1] += conv(1, 1)
    wait_halos(1, 1)
    shift(1)
    total[0] += conv(0, 1)
    total[1] += conv(1, 0)
    out_v[1] = (mixed[1].astype(f32) + total[1] + row(conv_bias)).astype(bf16)
    out_copy(1).start()
    wait_halos(0, 1)
    shift(0)
    out_v[0] = (
        mixed[0].astype(f32) + (total[0] + conv(0, 0)) + row(conv_bias)
    ).astype(bf16)

    out_copy(0).start()

    for f in (1, 0):
        out_copy(f).wait()
    for f in (1, 0):
        for step in range(1, steps + 1):
            for way in (0, 1):
                for part in parts_of(way, step):
                    ring_copy(f, way, step, part).wait_send()
        for offset in range(H):
            for part in (0, 1):
                for j in range(1, W):
                    side_copy(f, offset, part, j).wait_send()
        for index, move in enumerate(MOVES):
            @pl.when(inside(*move))
            def _():
                halo_copy(f, index).wait_send()


def shards(
    mesh_sizes,
    frames,
    attn_gain,
    qkv_weight,
    proj_weight,
    proj_bias,
    conv_gain,
    conv_weight,
    conv_bias,
):
    T, H, W = mesh_sizes
    frame_count, rows, cols, channels = frames.shape
    cells = rows * cols
    blocks = H * W
    group = math.gcd(blocks, 8)
    anywhere = pl.BlockSpec(memory_space=pl.ANY)
    dma = pltpu.SemaphoreType.DMA
    steps = max(H // 2, 1)
    limit = 60 << 20
    decoded = pl.pallas_call(
        functools.partial(kernel, (T, H, W, rows, cols, channels)),
        out_shape=jax.ShapeDtypeStruct((frame_count, cells, channels), bf16),
        in_specs=[pl.BlockSpec(memory_space=pltpu.HBM)] * 8,
        out_specs=anywhere,
        scratch_shapes=[
            pltpu.VMEM((channels,), f32),
            pltpu.VMEM((channels,), f32),
            pltpu.VMEM((channels,), f32),
            pltpu.VMEM((channels,), f32),
            pltpu.VMEM((2, cells, channels), bf16),
            pltpu.VMEM((2, cells, channels), bf16),
            pltpu.VMEM((channels, 3 * channels), bf16),
            pltpu.VMEM((channels, channels), bf16),
            pltpu.VMEM((9, 3 * channels, channels), bf16),
            pltpu.VMEM((2, blocks, cells, channels), bf16),
            pltpu.VMEM((2, cells, channels), bf16),
            pltpu.VMEM((channels, channels), bf16),
            pltpu.VMEM((cells, blocks * cells), f32),
            pltpu.VMEM((cells, group * cells), bf16),
            pltpu.VMEM((channels // lanes, cells, lanes), f32),
            pltpu.VMEM((2, cells, channels), bf16),
            pltpu.VMEM((4, (rows + 2) * cols, channels), bf16),
            pltpu.VMEM((4, 2, rows, channels), bf16),
            pltpu.VMEM((4, 4, cols, channels), bf16),
            pltpu.VMEM((2, 2, rows, channels), bf16),
            pltpu.VMEM((4, (rows + 2) * cols, 3 * channels), bf16),
            pltpu.VMEM((2, cells, channels), f32),
            dma((7,)),
            dma((2,)),
            dma((3,)),
            dma((2, 2, steps, 2)),
            dma((2, 2, steps, 2)),
            dma((2, H, 2, W)),
            dma((2, H, 2, W)),
            dma((2, len(MOVES))),
            dma((2, len(MOVES))),
        ],
        compiler_params=pltpu.CompilerParams(
            collective_id=0, has_side_effects=True, vmem_limit_bytes=limit
        ),
    )(
        frames.reshape(frame_count, cells, channels),
        qkv_weight,
        proj_weight,
        conv_weight.reshape(9, 3 * channels, channels),
        attn_gain,
        proj_bias,
        conv_gain,
        conv_bias,
    )
    return decoded.reshape(frame_count, rows, cols, channels)


def solution(mesh):
    sizes = tuple(mesh.shape[axis] for axis in ("tm", "height", "width"))
    in_specs = (P("tm", "height", "width", None), P(), P(), P(), P(), P(), P(), P())
    out_specs = P("tm", "height", "width", None)
    return jax.shard_map(
        functools.partial(shards, sizes),
        mesh=mesh,
        in_specs=in_specs,
        out_specs=out_specs,
        check_vma=False,
    )
```

```python
import functools
import math

import jax
import jax.numpy as jnp
from jax import lax
from jax.experimental import pallas as pl
from jax.experimental.pallas import tpu as pltpu
from jax.sharding import PartitionSpec as P

epsilon = 1e-06
MESH = pl.DeviceIdType.MESH
f32 = jnp.float32
bf16 = jnp.bfloat16
lanes = 128

MOVES = [
    (dt, dh, dw)
    for dt in (1, 0)
    for dh in (-1, 1, 0)
    for dw in (-1, 1, 0)
    if (dt, dh, dw) != (0, 0, 0)
]
CORNERS = {(-1, -1): 0, (-1, 1): 1, (1, -1): 2, (1, 1): 3}


def dot(a, b):
    return jnp.dot(a, b, preferred_element_type=f32)


def dot_t(a, b):
    return lax.dot_general(a, b, (((1,), (1,)), ((), ())), preferred_element_type=f32)


def row(vector):
    return vector[...].reshape(1, vector.shape[0])


def rms(values, gain_row):
    mean_square = jnp.mean(values * values, axis=-1, keepdims=True)
    return values * lax.rsqrt(mean_square + epsilon) * gain_row


def kernel(
    sizes,
    frames_hbm,
    qkv_hbm,
    proj_hbm,
    convw_hbm,
    attn_gain_hbm,
    proj_bias_hbm,
    conv_gain_hbm,
    conv_bias_hbm,
    out_hbm,
    attn_gain,
    proj_bias,
    conv_gain,
    conv_bias,
    out_v,
    frames_v,
    qkv_v,
    proj_v,
    convw_v,
    gathered,
    query,
    value_proj,
    scores,
    weights,
    conv_f32,
    mixed,
    centre,
    columns,
    corners,
    edge,
    shifted,
    total,
    load_sem,
    out_sem,
    convw_sem,
    ring_send,
    ring_recv,
    side_send,
    side_recv,
    halo_send,
    halo_recv,
):
    T, H, W, rows, cols, channels = sizes
    cells = rows * cols
    half = cells // 2
    blocks = H * W
    t, h, w = lax.axis_index("tm"), lax.axis_index("height"), lax.axis_index("width")

    loads = [
        pltpu.make_async_copy(frames_hbm, frames_v, load_sem.at[0]),
        pltpu.make_async_copy(attn_gain_hbm, attn_gain, load_sem.at[1]),
        pltpu.make_async_copy(qkv_hbm, qkv_v, load_sem.at[2]),
        pltpu.make_async_copy(proj_hbm, proj_v, load_sem.at[3]),
        pltpu.make_async_copy(proj_bias_hbm, proj_bias, load_sem.at[4]),
        pltpu.make_async_copy(conv_gain_hbm, conv_gain, load_sem.at[5]),
        pltpu.make_async_copy(conv_bias_hbm, conv_bias, load_sem.at[6]),
    ]
    for copy in loads:
        copy.start()
    convw_loads = [
        pltpu.make_async_copy(convw_hbm.at[pl.ds(3 * a, 3)], convw_v.at[pl.ds(3 * a, 3)], convw_sem.at[a])
        for a in range(3)
    ]

    square = H == 4 and W == 2

    def turn(p):
        return p + (p // 2) * (1 - 2 * (p % 2)) if square else p

    pos = turn(h)

    def at_pos(offset):
        return turn((pos + offset + H) % H)

    def device(dt, hh, ww):
        return {"tm": t + dt, "height": hh, "width": ww}

    def inside(dt, dh, dw):
        ok = None
        for value, delta, count in ((t, dt, T), (h, dh, H), (w, dw, W)):
            if delta:
                one = value + delta < count if delta > 0 else value + delta >= 0
                ok = one if ok is None else jnp.logical_and(ok, one)
        return ok

    centre[...] = jnp.zeros_like(centre)
    columns[...] = jnp.zeros_like(columns)
    corners[...] = jnp.zeros_like(corners)

    barrier = pltpu.get_barrier_semaphore()

    def greet(target):
        pl.semaphore_signal(barrier, inc=1, device_id=target, device_id_type=MESH)

    close = 0
    if H > 1:
        greet(device(0, at_pos(1), w))
        greet(device(0, at_pos(-1), w))
        close += 2
    for j in range(1, W):
        greet(device(0, h, (w + j) % W))
        close += 1
    for dt, dh, dw in MOVES:
        @pl.when(inside(-dt, -dh, -dw))
        def _():
            greet(device(-dt, h - dh, w - dw))

    own = h * W + w
    loads[0].wait()
    loads[1].wait()
    for f in (1, 0):
        gathered[f, own] = rms(frames_v[f].astype(f32), row(attn_gain)).astype(bf16)

    def count(delta, value, limit):
        one = value + delta < limit if delta > 0 else value + delta >= 0
        return jnp.where(one, 1, 0)

    around = (1 + count(1, h, H) + count(-1, h, H)) * (1 + count(1, w, W) + count(-1, w, W))
    pl.semaphore_wait(barrier, close + around - 1 + count(1, t, T) * around)

    def ring_copy(f, way, step, part):
        sign = 1 if way == 0 else -1
        origin = at_pos(-sign * (step - 1))
        piece = gathered.at[f, origin * W + w, pl.ds(part * half, half)]
        return pltpu.make_async_remote_copy(
            piece,
            piece,
            ring_send.at[f, way, step - 1, part],
            ring_recv.at[f, way, step - 1, part],
            device_id=device(0, at_pos(sign), w),
            device_id_type=MESH,
        )

    def ring_arrival(f, way, step, part):
        sign = 1 if way == 0 else -1
        origin = at_pos(-sign * step)
        piece = gathered.at[f, origin * W + w, pl.ds(part * half, half)]
        return pltpu.make_async_remote_copy(
            piece,
            piece,
            ring_send.at[f, way, step - 1, part],
            ring_recv.at[f, way, step - 1, part],
            device_id=device(0, at_pos(sign), w),
            device_id_type=MESH,
        )

    def parts_of(way, step):
        if 2 * step < H:
            return (0, 1) if way == 0 else (1, 0)
        return (way,)

    def side_copy(f, offset, part, j, incoming=False):
        column = (w - j + W) % W if incoming else w
        piece = gathered.at[f, at_pos(-offset) * W + column, pl.ds(part * half, half)]
        return pltpu.make_async_remote_copy(
            piece,
            piece,
            side_send.at[f, offset, part, j],
            side_recv.at[f, offset, part, j],
            device_id=device(0, h, (w + j) % W),
            device_id_type=MESH,
        )

    def pass_aside(f, offset, part):
        for j in range(1, W):
            side_copy(f, offset, part, j).start()

    steps = H // 2

    def start_own(f):
        if H > 1:
            for k in range(len(parts_of(0, 1))):
                for way in (0, 1):
                    ring_copy(f, way, 1, parts_of(way, 1)[k]).start()
        for part in (0, 1):
            pass_aside(f, 0, part)

    def arrive(f, way, step, k):
        part = parts_of(way, step)[k]
        ring_arrival(f, way, step, part).wait_recv()
        if step < steps and part in parts_of(way, step + 1):
            ring_copy(f, way, step + 1, part).start()
        pass_aside(f, step if way == 0 else H - step, part)

    arrivals = [
        (step, k, way)
        for step in range(1, steps + 1)
        for k in range(len(parts_of(0, step)))
        for way in (0, 1)
    ]

    def finish_gather(f):
        for offset in range(H):
            for part in (0, 1):
                for j in range(1, W):
                    side_copy(f, offset, part, j, incoming=True).wait_recv()

    start_own(1)
    for copy in convw_loads:
        copy.start()

    for copy in loads[2:]:
        copy.wait()
    value_proj[...] = dot(qkv_v[:, 2 * channels :], proj_v[...]).astype(bf16)
    score_scale = 1.0 / math.sqrt(channels)
    for f in (1, 0):
        q = dot(gathered[f, own], qkv_v[:, :channels]).astype(bf16)
        query[f] = (dot_t(q, qkv_v[:, channels : 2 * channels]) * score_scale).astype(bf16)

    group = math.gcd(blocks, 8)

    def attend(f):
        q = query[f]
        lane_max = None
        for j in range(blocks):
            s = dot_t(q, gathered[f, j])
            scores[:, j * cells : (j + 1) * cells] = s
            for c in range(0, cells, lanes):
                part = s[:, c : c + lanes]
                lane_max = part if lane_max is None else jnp.maximum(lane_max, part)
        row_max = jnp.max(lane_max, axis=-1, keepdims=True)
        lane_sum = None
        summed = None
        for g in range(0, blocks, group):
            for j in range(g, g + group):
                p = jnp.exp(scores[:, j * cells : (j + 1) * cells] - row_max)
                for c in range(0, cells, lanes):
                    part = p[:, c : c + lanes]
                    lane_sum = part if lane_sum is None else lane_sum + part
                weights[:, (j - g) * cells : (j - g + 1) * cells] = p.astype(bf16)
            keys = gathered[f, pl.ds(g, group)].reshape(group * cells, channels)
            one = dot(weights[...], keys)
            summed = one if summed is None else summed + one
        row_sum = jnp.sum(lane_sum, axis=-1, keepdims=True)
        context = (summed / row_sum).astype(bf16)
        projected = dot(context, value_proj[...])
        now = (frames_v[f].astype(f32) + projected + row(proj_bias)).astype(bf16)
        mixed[f] = now
        v = rms(now.astype(f32), row(conv_gain))
        c_in = v / (1.0 + jnp.exp(-v))
        centre[2 + f, pl.ds(cols, cells)] = c_in.astype(bf16)
        for c in range(channels // lanes):
            span = slice(c * lanes, (c + 1) * lanes)
            conv_f32[c] = c_in[:, span]
            edge[f, 0, :, span] = conv_f32[c, pl.ds(0, rows, cols), :].astype(bf16)
            edge[f, 1, :, span] = conv_f32[c, pl.ds(cols - 1, rows, cols), :].astype(bf16)

    def halo_copy(f, index):
        dt, dh, dw = MOVES[index]
        slot = f if dt else 2 + f
        row = {0: cols, -1: cols, 1: rows * cols}[dh]
        if dh == 0 and dw == 0:
            src = centre.at[2 + f, pl.ds(cols, cells)]
            dst = centre.at[slot, pl.ds(cols, cells)]
        elif dw == 0:
            src = centre.at[2 + f, pl.ds(row, cols)]
            dst = centre.at[slot, pl.ds((rows + 1) * cols if dh < 0 else 0, cols)]
        elif dh == 0:
            src = edge.at[f, 0 if dw < 0 else 1]
            dst = columns.at[slot, 1 if dw < 0 else 0]
        else:
            src = centre.at[2 + f, pl.ds(row, cols)]
            dst = corners.at[slot, CORNERS[(-dh, -dw)]]
        return pltpu.make_async_remote_copy(
            src,
            dst,
            halo_send.at[f, index],
            halo_recv.at[f, index],
            device_id=device(dt, h + dh, w + dw),
            device_id_type=MESH,
        )

    def send_halos(f):
        for index, move in enumerate(MOVES):
            @pl.when(inside(*move))
            def _():
                halo_copy(f, index).start()

    def wait_halos(f, ahead):
        for index, (dt, dh, dw) in enumerate(MOVES):
            if dt == ahead:
                @pl.when(inside(-dt, -dh, -dw))
                def _():
                    halo_copy(f, index).wait_recv()

    def shift(s):
        place = lax.broadcasted_iota(jnp.int32, (cols, channels), 0)
        first, last = place == 0, place == cols - 1
        low, high = columns[s, 0].astype(f32), columns[s, 1].astype(f32)
        for r in range(rows + 2):
            here = centre[s, r * cols : (r + 1) * cols]
            x = here.astype(f32)
            if 0 < r <= rows:
                before, after = low[r - 1 : r], high[r - 1 : r]
            else:
                c = 0 if r == 0 else 2
                before = corners[s, c].astype(f32)[cols - 1 : cols]
                after = corners[s, c + 1].astype(f32)[0:1]
            there = pl.ds(r * cols, cols)
            shifted[s, there, 0:channels] = jnp.where(
                first, before, pltpu.roll(x, 1, axis=0)
            ).astype(bf16)
            shifted[s, there, channels : 2 * channels] = here
            shifted[s, there, 2 * channels : 3 * channels] = jnp.where(
                last, after, pltpu.roll(x, cols - 1, axis=0)
            ).astype(bf16)

    def conv(o, a):
        s = o + a
        value = None
        for b in range(3):
            one = dot(shifted[s, b * cols : b * cols + cells], convw_v[3 * a + b])
            value = one if value is None else value + one
        return value

    def out_copy(f):
        return pltpu.make_async_copy(out_v.at[f], out_hbm.at[f], out_sem.at[f])

    early = 2 if steps > 1 else 0
    for step, k, way in arrivals[:early]:
        arrive(1, way, step, k)
    start_own(0)
    for step, k, way in arrivals[early:]:
        arrive(1, way, step, k)
    finish_gather(1)
    for step, k, way in arrivals[:early]:
        arrive(0, way, step, k)
    attend(1)
    send_halos(1)
    for copy in convw_loads:
        copy.wait()
    for step, k, way in arrivals[early : 2 * early]:
        arrive(0, way, step, k)
    wait_halos(1, 0)
    shift(3)
    total[1] = conv(1, 2)
    for step, k, way in arrivals[2 * early :]:
        arrive(0, way, step, k)
    finish_gather(0)
    attend(0)
    send_halos(0)
    wait_halos(0, 0)
    shift(2)
    total[0] = conv(0, 2)
    total[1] += conv(1, 1)
    wait_halos(1, 1)
    shift(1)
    total[0] += conv(0, 1)
    total[1] += conv(1, 0)
    out_v[1] = (mixed[1].astype(f32) + total[1] + row(conv_bias)).astype(bf16)
    out_copy(1).start()
    wait_halos(0, 1)
    shift(0)
    out_v[0] = (
        mixed[0].astype(f32) + (total[0] + conv(0, 0)) + row(conv_bias)
    ).astype(bf16)

    out_copy(0).start()

    for f in (1, 0):
        out_copy(f).wait()
    for f in (1, 0):
        for step in range(1, steps + 1):
            for way in (0, 1):
                for part in parts_of(way, step):
                    ring_copy(f, way, step, part).wait_send()
        for offset in range(H):
            for part in (0, 1):
                for j in range(1, W):
                    side_copy(f, offset, part, j).wait_send()
        for index, move in enumerate(MOVES):
            @pl.when(inside(*move))
            def _():
                halo_copy(f, index).wait_send()


def shards(
    mesh_sizes,
    frames,
    attn_gain,
    qkv_weight,
    proj_weight,
    proj_bias,
    conv_gain,
    conv_weight,
    conv_bias,
):
    T, H, W = mesh_sizes
    frame_count, rows, cols, channels = frames.shape
    cells = rows * cols
    blocks = H * W
    group = math.gcd(blocks, 8)
    anywhere = pl.BlockSpec(memory_space=pl.ANY)
    dma = pltpu.SemaphoreType.DMA
    steps = max(H // 2, 1)
    limit = 60 << 20
    decoded = pl.pallas_call(
        functools.partial(kernel, (T, H, W, rows, cols, channels)),
        out_shape=jax.ShapeDtypeStruct((frame_count, cells, channels), bf16),
        in_specs=[pl.BlockSpec(memory_space=pltpu.HBM)] * 8,
        out_specs=anywhere,
        scratch_shapes=[
            pltpu.VMEM((channels,), f32),
            pltpu.VMEM((channels,), f32),
            pltpu.VMEM((channels,), f32),
            pltpu.VMEM((channels,), f32),
            pltpu.VMEM((2, cells, channels), bf16),
            pltpu.VMEM((2, cells, channels), bf16),
            pltpu.VMEM((channels, 3 * channels), bf16),
            pltpu.VMEM((channels, channels), bf16),
            pltpu.VMEM((9, 3 * channels, channels), bf16),
            pltpu.VMEM((2, blocks, cells, channels), bf16),
            pltpu.VMEM((2, cells, channels), bf16),
            pltpu.VMEM((channels, channels), bf16),
            pltpu.VMEM((cells, blocks * cells), f32),
            pltpu.VMEM((cells, group * cells), bf16),
            pltpu.VMEM((channels // lanes, cells, lanes), f32),
            pltpu.VMEM((2, cells, channels), bf16),
            pltpu.VMEM((4, (rows + 2) * cols, channels), bf16),
            pltpu.VMEM((4, 2, rows, channels), bf16),
            pltpu.VMEM((4, 4, cols, channels), bf16),
            pltpu.VMEM((2, 2, rows, channels), bf16),
            pltpu.VMEM((4, (rows + 2) * cols, 3 * channels), bf16),
            pltpu.VMEM((2, cells, channels), f32),
            dma((7,)),
            dma((2,)),
            dma((3,)),
            dma((2, 2, steps, 2)),
            dma((2, 2, steps, 2)),
            dma((2, H, 2, W)),
            dma((2, H, 2, W)),
            dma((2, len(MOVES))),
            dma((2, len(MOVES))),
        ],
        compiler_params=pltpu.CompilerParams(
            collective_id=0, has_side_effects=True, vmem_limit_bytes=limit
        ),
    )(
        frames.reshape(frame_count, cells, channels),
        qkv_weight,
        proj_weight,
        conv_weight.reshape(9, 3 * channels, channels),
        attn_gain,
        proj_bias,
        conv_gain,
        conv_bias,
    )
    return decoded.reshape(frame_count, rows, cols, channels)


def solution(mesh):
    sizes = tuple(mesh.shape[axis] for axis in ("tm", "height", "width"))
    in_specs = (P("tm", "height", "width", None), P(), P(), P(), P(), P(), P(), P())
    out_specs = P("tm", "height", "width", None)
    return jax.shard_map(
        functools.partial(shards, sizes),
        mesh=mesh,
        in_specs=in_specs,
        out_specs=out_specs,
        check_vma=False,
    )
```
